512 devices in a mesh: team: 32 (over x_hi, y, core), rep: 16 (over x_lo, z).
Axes of the slice: x: 4 (x_hi: 2, x_lo: 2; x = x_hi * 2 + x_lo), y: 8, z: 8, core: 2. Of those that a mesh axis runs over, the one named last changes fastest.
Arguments:
- points: bfloat16 [32768, 128], P('team'), may hold values from -3 to 3
Outputs:
- potential: float32 [32768], P('team')
- displacement: float32 [32768, 128], P('team')
The draws below stay inside these ranges and needn't reach their ends.
All inputs are finite; a program needn't handle non-finite values.
Results may differ from the reference program's by a relative error of at most 0.0097.
The reference program's roundings to bfloat16 on the way (of `rounded`) count: a program that leaves them out, or rounds other values in their place, can miss the bound.
Values may be sent and summed in bfloat16 or wider, within the bound.
A program may use at most 64 MiB of HBM per device.

```python
import math
import jax
import jax.numpy as jnp
from jax import lax

D = 128
TEAM_PTS = 1024
NPTS = 32768
N_TEAM = 32


def draw_points(key, part):
    base_key = jax.random.fold_in(key, 11)
    scale_key = jax.random.fold_in(key, 23)
    center_key = jax.random.fold_in(key, 37)
    label_key = jax.random.fold_in(key, 41)
    clusters = 8
    labels = jax.random.randint(label_key, (NPTS,), 0, clusters)
    centers = jax.random.normal(center_key, (clusters, D), jnp.float32) * 0.3
    values = jax.random.normal(base_key, (NPTS, D), jnp.float32)
    scales = jnp.exp(jax.random.uniform(scale_key, (NPTS, 1), jnp.float32, -0.35, 0.35))
    noise = values * scales * (2.8 / math.sqrt(D))
    shared = jnp.take(centers, labels, axis=0)
    return jnp.clip(shared + noise, -3.0, 3.0).astype(jnp.bfloat16)


def setup_inputs(seed: int = 0) -> dict:
    keys = jax.random.split(jax.random.key(seed), 2)
    points = draw_points(jax.random.fold_in(keys[1], 71), 0)
    return dict(points=points)


def row_sums(points_wide, sq_norm, potentials, inv_eps, with_num):
    blocks = points_wide.reshape(N_TEAM, TEAM_PTS, D)
    sq_blocks = sq_norm.reshape(N_TEAM, TEAM_PTS)

    def one_block(inputs):
        row_points, row_sq = inputs
        products = jnp.dot(row_points, points_wide.T, precision=lax.Precision.HIGHEST, preferred_element_type=jnp.float32)
        cost_tile = 0.5 * row_sq[:, None] + 0.5 * sq_norm[None, :] - products
        kernel = jnp.exp((potentials[None, :] - cost_tile) * inv_eps)
        row_total = jnp.sum(kernel, axis=1)
        if with_num:
            rounded = lax.optimization_barrier(kernel.astype(jnp.bfloat16)).astype(jnp.float32)
            numerator = jnp.dot(rounded, points_wide, precision=lax.Precision.HIGHEST, preferred_element_type=jnp.float32)
            return row_total, numerator
        return row_total, row_total

    totals, numerators = lax.map(one_block, (blocks, sq_blocks))
    if with_num:
        return totals.reshape(NPTS), numerators.reshape(NPTS, D)
    return totals.reshape(NPTS), totals.reshape(NPTS)


def reference(points):
    points_wide = points.astype(jnp.float32)
    sq_norm = jnp.sum(points_wide * points_wide, axis=1)
    log_count = jnp.log(jnp.float32(NPTS))
    zero_pot = jnp.zeros((NPTS,), jnp.float32)
    first_sum, unused_rows = row_sums(points_wide, sq_norm, zero_pot, 0.25, False)
    pot_one = 0.5 * (zero_pot - 4.0 * (jnp.log(first_sum) - log_count))
    second, numerator = row_sums(points_wide, sq_norm, pot_one, 0.5, True)
    potential = 0.5 * (pot_one - 2.0 * (jnp.log(second) - log_count))
    displacement = points_wide - numerator / second[:, None]
    return potential, displacement
```

```python
import jax
import jax.numpy as jnp
from jax import lax
from jax.sharding import PartitionSpec as P


def shards(points):
    rows, width = points.shape
    replicas = lax.axis_size("rep")
    teams = lax.axis_size("team")
    part = rows // replicas
    replica = lax.axis_index("rep")
    log_count = jnp.log(jnp.float32(rows * teams))

    mine = lax.dynamic_slice_in_dim(points, replica * part, part, 0)
    cols = lax.all_gather(mine, "team", axis=0, tiled=True)
    half_rows = 0.5 * jnp.sum(jnp.square(points.astype(jnp.float32)), axis=1)
    half_cols = 0.5 * jnp.sum(jnp.square(cols.astype(jnp.float32)), axis=1)
    products = lax.dot_general(
        points, cols, (((1,), (1,)), ((), ())), preferred_element_type=jnp.float32
    )
    cost = half_rows[:, None] + half_cols[None, :] - products
    first = lax.psum(jnp.sum(jnp.exp(cost * -0.25), axis=1), "rep")
    pot_one = -2.0 * (jnp.log(first) - log_count)
    pot_mine = lax.dynamic_slice_in_dim(pot_one, replica * part, part, 0)
    pot_cols = lax.all_gather(pot_mine, "team", axis=0, tiled=True)
    kernel = jnp.exp((pot_cols[None, :] - cost) * 0.5)
    second_part = jnp.sum(kernel, axis=1)
    numer_part = jnp.dot(
        kernel.astype(jnp.bfloat16), cols, preferred_element_type=jnp.float32
    )
    second, numer = lax.psum((second_part, numer_part), "rep")
    potential = 0.5 * (pot_one - 2.0 * (jnp.log(second) - log_count))
    displacement = points.astype(jnp.float32) - numer / second[:, None]
    return (potential, displacement)


def solution(mesh):
    return jax.shard_map(
        shards,
        mesh=mesh,
        in_specs=(P("team", None),),
        out_specs=(P("team"), P("team", None)),
        check_vma=False,
    )
```

```python
import functools
import math

import jax
import jax.numpy as jnp
from jax import lax
from jax.experimental import pallas as pl
from jax.experimental.pallas import tpu as pltpu
from jax.sharding import PartitionSpec as P

LANES = 128
PART = 64
MESH = pl.DeviceIdType.MESH
LOG2E = math.log2(math.e)


def split3(value):
    high = value.astype(jnp.bfloat16).astype(jnp.float32)
    rest = value - high
    mid = rest.astype(jnp.bfloat16).astype(jnp.float32)
    return high, mid, rest - mid


def extra_lanes(block, first, ones):
    wide = block.astype(jnp.float32)
    half = -0.5 * jnp.sum(wide * wide, axis=1, keepdims=True)
    high, mid, low = split3(half)
    lane = lax.broadcasted_iota(jnp.int32, wide.shape, 1)
    extra = jnp.where((lane >= ones) & (lane < ones + 3), 1.0, 0.0)
    extra = jnp.where(lane == first, high, extra)
    extra = jnp.where(lane == first + 1, mid, extra)
    extra = jnp.where(lane == first + 2, low, extra)
    return extra.astype(jnp.bfloat16)


def row_of(acc):
    size = acc.shape[0]
    total = jnp.sum(acc, axis=1, keepdims=True)
    lane = lax.broadcasted_iota(jnp.int32, (size, LANES), 1)
    sub = lax.broadcasted_iota(jnp.int32, (size, LANES), 0)
    return jnp.sum(jnp.where(lane == sub, total, 0.0), axis=0, keepdims=True)


def body(
    teams, reps, pts, pot_out, disp_out,
    rows_aug, cols, cols_aug, sum_one, got_one, pot_mine, pot_cols, pot_rows,
    sum_two, got_two, numer, got_numer, disp_mine, pot_all,
    send_sem, local_sem, rv_pts, rv_one, rv_pot, rv_two, rv_num, rv_disp, rv_fin,
):
    rows = pts.shape[0]
    blocks = rows // LANES
    ncols = teams * PART
    log_count = math.log(rows * teams)
    t = lax.axis_index("team")
    r = lax.axis_index("rep")
    half = lax.rem(r, 2)
    nt = (((1,), (1,)), ((), ()))

    def team_peer(k):
        return lax.rem(t + k, teams)

    def rep_peer(k):
        return lax.rem(r + k, reps)

    def part_at(index):
        return pl.ds(pl.multiple_of(index * PART, PART), PART)

    def block_at(index):
        return pl.ds(pl.multiple_of(index * LANES, LANES), LANES)

    def remote(src, dst, send, recv, where):
        return pltpu.make_async_remote_copy(
            src_ref=src, dst_ref=dst, send_sem=send, recv_sem=recv,
            device_id=where, device_id_type=MESH,
        )

    def each(count, step):
        lax.fori_loop(1, count, lambda k, c: (step(k), c)[1], 0)

    barrier = pltpu.get_barrier_semaphore()

    def greet_team(k):
        pl.semaphore_signal(barrier, 1, device_id={"team": team_peer(k)}, device_id_type=MESH)

    def greet_rep(k):
        pl.semaphore_signal(barrier, 1, device_id={"rep": rep_peer(k)}, device_id_type=MESH)

    each(teams, greet_team)
    each(reps, greet_rep)

    cols[part_at(t), :] = pts[part_at(r), :]

    def widen_rows(b, carry):
        block = pts[block_at(b), :]
        rows_aug[block_at(b), pl.ds(0, LANES)] = block
        rows_aug[block_at(b), pl.ds(LANES, LANES)] = extra_lanes(block, 0, 3)
        return carry

    lax.fori_loop(0, blocks, widen_rows, 0)
    pl.semaphore_wait(barrier, teams + reps - 2)

    def points_copy(k, owner):
        return remote(
            pts.at[part_at(r), :], cols.at[part_at(owner), :],
            send_sem.at[0], rv_pts.at[owner], {"team": team_peer(k)},
        )

    each(teams, lambda k: points_copy(k, t).start())
    each(teams, lambda k: points_copy(k, team_peer(k)).wait_recv())

    def widen_cols(b, carry):
        block = cols[block_at(b), :]
        cols_aug[block_at(b), pl.ds(0, LANES)] = block
        cols_aug[block_at(b), pl.ds(LANES, LANES)] = extra_lanes(block, 3, 0)
        return carry

    lax.fori_loop(0, ncols // LANES, widen_cols, 0)

    def first_block(b, carry):
        mine = rows_aug[block_at(b), :]
        acc = jnp.zeros((LANES, LANES), jnp.float32)
        for s in range(ncols // 256):
            tile = lax.dot_general(
                mine, cols_aug[pl.ds(s * 256, 256), :], nt, preferred_element_type=jnp.float32
            )
            tile = jnp.exp2(tile * (0.25 * LOG2E))
            acc = acc + tile[:, :LANES] + tile[:, LANES:]
        sum_one[b] = row_of(acc)
        return carry

    lax.fori_loop(0, blocks, first_block, 0)

    def one_copy(k, owner):
        return remote(
            sum_one.at[rep_peer(k) // 2], got_one.at[owner],
            send_sem.at[1], rv_one.at[owner], {"rep": rep_peer(k)},
        )

    each(reps, lambda k: one_copy(k, r).start())
    got_one[r] = sum_one[r // 2]
    each(reps, lambda k: one_copy(k, rep_peer(k)).wait_recv())
    first = got_one[0]
    for q in range(1, reps):
        first = first + got_one[q]
    pot_one = -2.0 * (jnp.log(first) - log_count)
    pot_mine[0] = pot_one

    def pot_copy(k, owner):
        return remote(
            pot_mine.at[0], pot_cols.at[owner],
            send_sem.at[2], rv_pot.at[owner], {"team": team_peer(k)},
        )

    each(teams, lambda k: pot_copy(k, t).start())
    pot_cols[t] = pot_one
    each(teams, lambda k: pot_copy(k, team_peer(k)).wait_recv())
    low_lane = lax.broadcasted_iota(jnp.int32, (1, LANES), 1) < PART
    upper = half == 1
    for s in range(teams // 2):
        even = pot_cols[2 * s]
        odd = pot_cols[2 * s + 1]
        even = jnp.where(upper, pltpu.roll(even, PART, 1), even)
        odd = jnp.where(upper, odd, pltpu.roll(odd, PART, 1))
        pot_rows[s] = jnp.where(low_lane, even, odd) * (0.5 * LOG2E)

    def two_copy(block, q, owner):
        return remote(
            sum_two.at[block], got_two.at[owner],
            send_sem.at[3], rv_two.at[owner], {"rep": q},
        )

    def numer_copy(q, owner):
        return remote(
            numer.at[part_at(q), :], got_numer.at[owner],
            send_sem.at[4], rv_num.at[owner], {"rep": q},
        )

    def second_block(i, carry):
        b = lax.rem(r // 2 + 1 + i, blocks)
        mine = rows_aug[block_at(b), :]
        acc = jnp.zeros((LANES, LANES), jnp.float32)
        total = jnp.zeros((LANES, LANES), jnp.float32)
        for s in range(ncols // 256):
            tile = lax.dot_general(
                mine, cols_aug[pl.ds(s * 256, 256), :], nt, preferred_element_type=jnp.float32
            )
            left = jnp.exp2(tile[:, :LANES] * (0.5 * LOG2E) + pot_rows[2 * s])
            right = jnp.exp2(tile[:, LANES:] * (0.5 * LOG2E) + pot_rows[2 * s + 1])
            acc = acc + left + right
            rounded = jnp.concatenate(
                [left.astype(jnp.bfloat16), right.astype(jnp.bfloat16)], axis=1
            )
            total = total + jnp.dot(
                rounded, cols[pl.ds(s * 256, 256), :], preferred_element_type=jnp.float32
            )
        numer[block_at(b), :] = total
        sum_two[b] = row_of(acc)
        for h in range(2):
            q = 2 * b + h

            @pl.when(q != r)
            def _():
                two_copy(b, q, r).start()
                numer_copy(q, r).start()

        return carry

    lax.fori_loop(0, blocks, second_block, 0)
    got_two[r] = sum_two[r // 2]
    got_numer[r] = numer[part_at(r), :]
    each(reps, lambda k: two_copy(0, rep_peer(k), rep_peer(k)).wait_recv())
    second = got_two[0]
    for q in range(1, reps):
        second = second + got_two[q]
    pot_all[r] = 0.5 * (pot_one - 2.0 * (jnp.log(second) - log_count))

    def fin_copy(k, owner):
        return remote(
            pot_all.at[r], pot_all.at[owner],
            send_sem.at[5], rv_fin.at[owner], {"rep": rep_peer(k)},
        )

    each(reps, lambda k: fin_copy(k, r).start())
    lane = lax.broadcasted_iota(jnp.int32, (PART, LANES), 1)
    sub = lax.broadcasted_iota(jnp.int32, (PART, LANES), 0)
    divisor = jnp.sum(jnp.where(lane == sub + half * PART, second, 0.0), axis=1, keepdims=True)
    each(reps, lambda k: numer_copy(rep_peer(k), rep_peer(k)).wait_recv())
    weighted = got_numer[0]
    for q in range(1, reps):
        weighted = weighted + got_numer[q]
    disp_mine[...] = pts[part_at(r), :].astype(jnp.float32) - weighted / divisor

    def disp_copy(k, owner):
        return remote(
            disp_mine, disp_out.at[part_at(owner), :],
            send_sem.at[6], rv_disp.at[owner], {"rep": rep_peer(k)},
        )

    each(reps, lambda k: disp_copy(k, r).start())
    keep = pltpu.make_async_copy(disp_mine, disp_out.at[part_at(r), :], local_sem)
    keep.start()
    each(reps, lambda k: fin_copy(k, rep_peer(k)).wait_recv())
    for b in range(blocks):
        pot_out[b] = pot_all[2 * b]
    each(teams, lambda k: points_copy(k, t).wait_send())
    each(reps, lambda k: one_copy(k, r).wait_send())
    each(teams, lambda k: pot_copy(k, t).wait_send())
    each(reps, lambda k: two_copy(0, rep_peer(k), r).wait_send())
    each(reps, lambda k: numer_copy(rep_peer(k), r).wait_send())
    each(reps, lambda k: fin_copy(k, r).wait_send())
    each(reps, lambda k: disp_copy(k, r).wait_send())
    each(reps, lambda k: disp_copy(k, rep_peer(k)).wait_recv())
    keep.wait()


def shards(points):
    rows, width = points.shape
    teams = lax.axis_size("team")
    reps = lax.axis_size("rep")
    blocks = rows // LANES
    f32 = jnp.float32
    dma = pltpu.SemaphoreType.DMA
    vmem = pltpu.VMEM
    potential, displacement = pl.pallas_call(
        functools.partial(body, teams, reps),
        out_shape=(
            jax.ShapeDtypeStruct((blocks, 1, LANES), f32),
            jax.ShapeDtypeStruct((rows, width), f32),
        ),
        in_specs=[pl.BlockSpec(memory_space=pltpu.VMEM)],
        out_specs=(
            pl.BlockSpec(memory_space=pltpu.VMEM),
            pl.BlockSpec(memory_space=pl.ANY),
        ),
        scratch_shapes=[
            vmem((rows, 2 * width), jnp.bfloat16),
            vmem((teams * PART, width), jnp.bfloat16),
            vmem((teams * PART, 2 * width), jnp.bfloat16),
            vmem((blocks, 1, LANES), f32),
            vmem((reps, 1, LANES), f32),
            vmem((1, 1, LANES), f32),
            vmem((teams, 1, LANES), f32),
            vmem((teams // 2, 1, LANES), f32),
            vmem((blocks, 1, LANES), f32),
            vmem((reps, 1, LANES), f32),
            vmem((rows, width), f32),
            vmem((reps, PART, width), f32),
            vmem((PART, width), f32),
            vmem((reps, 1, LANES), f32),
            dma((7,)),
            dma,
            dma((teams,)),
            dma((reps,)),
            dma((teams,)),
            dma((reps,)),
            dma((reps,)),
            dma((reps,)),
            dma((reps,)),
        ],
        compiler_params=pltpu.CompilerParams(collective_id=0, has_side_effects=True),
    )(points)
    return potential.reshape(rows), displacement


def solution(mesh):
    return jax.shard_map(
        shards,
        mesh=mesh,
        in_specs=(P("team", None),),
        out_specs=(P("team"), P("team", None)),
        check_vma=False,
    )
```

```python
import functools
import math

import jax
import jax.numpy as jnp
from jax import lax
from jax.experimental import pallas as pl
from jax.experimental.pallas import tpu as pltpu
from jax.sharding import PartitionSpec as P

LANES = 128
PART = 64
MESH = pl.DeviceIdType.MESH
LOG2E = math.log2(math.e)


def split3(value):
    high = value.astype(jnp.bfloat16).astype(jnp.float32)
    rest = value - high
    mid = rest.astype(jnp.bfloat16).astype(jnp.float32)
    return high, mid, rest - mid


def extra_lanes(block, first, ones):
    wide = block.astype(jnp.float32)
    half = -0.5 * jnp.sum(wide * wide, axis=1, keepdims=True)
    high, mid, low = split3(half)
    lane = lax.broadcasted_iota(jnp.int32, wide.shape, 1)
    extra = jnp.where((lane >= ones) & (lane < ones + 3), 1.0, 0.0)
    extra = jnp.where(lane == first, high, extra)
    extra = jnp.where(lane == first + 1, mid, extra)
    extra = jnp.where(lane == first + 2, low, extra)
    return extra.astype(jnp.bfloat16)


def row_of(acc):
    size = acc.shape[0]
    total = jnp.sum(acc, axis=1, keepdims=True)
    lane = lax.broadcasted_iota(jnp.int32, (size, LANES), 1)
    sub = lax.broadcasted_iota(jnp.int32, (size, LANES), 0)
    return jnp.sum(jnp.where(lane == sub, total, 0.0), axis=0, keepdims=True)


def body(
    teams, reps, pts, pot_out, disp_out,
    rows_aug, cols, expo, part_one, sib_one, chip_one, got_one, pot, pot_scaled,
    numer, sum_two, far_numer, far_two, got_numer, got_two, disp_mine, pot_all,
    send_sem, local_sem, rv_pts, rv_fwd, rv_sib, rv_one, rv_pot,
    rv_xnum, rv_xtwo, rv_num, rv_two, rv_disp, rv_side, rv_fin,
):
    rows = pts.shape[0]
    blocks = rows // LANES
    ncols = teams * PART
    chunks = ncols // 256
    depth = reps // 2
    half_blocks = blocks // 2
    log_count = math.log(rows * teams)
    t = lax.axis_index("team")
    r = lax.axis_index("rep")
    core = lax.rem(t, 2)
    sibling = t + 1 - 2 * core
    near = r // depth
    z = lax.rem(r, depth)
    across = lax.rem(r + depth, reps)
    pairs = chunks // 2
    home = t // 4
    nt = (((1,), (1,)), ((), ()))

    def part_at(index):
        return pl.ds(pl.multiple_of(index * PART, PART), PART)

    def block_at(index):
        return pl.ds(pl.multiple_of(index * LANES, LANES), LANES)

    def chunk_at(index):
        return pl.ds(pl.multiple_of(index * 256, 256), 256)

    def remote(src, dst, send, recv, where):
        return pltpu.make_async_remote_copy(
            src_ref=src, dst_ref=dst, send_sem=send, recv_sem=recv,
            device_id=where, device_id_type=MESH,
        )

    def each(first, count, step):
        lax.fori_loop(first, count, lambda k, c: (step(k), c)[1], 0)

    def same_core(k):
        return lax.rem(t + 2 * k, teams)

    def rep_peer(k):
        return lax.rem(r + k, reps)

    def z_peer(k):
        return near * depth + lax.rem(z + k, depth)

    def chunk_of(i):
        side, step = lax.rem(i, 2), i // 2
        step = step + (step // 2) * (1 - 2 * lax.rem(step, 2))
        return lax.rem(home // pairs + side, 2) * pairs + lax.rem(home + step, pairs)

    chips = teams // 2
    pend = []

    def finish():
        for step in pend:
            step()

    barrier = pltpu.get_barrier_semaphore()

    def greet(where):
        pl.semaphore_signal(barrier, 1, device_id=where, device_id_type=MESH)

    each(1, chips, lambda k: greet({"team": same_core(k)}))
    greet({"team": sibling})
    each(1, reps, lambda k: greet({"rep": rep_peer(k)}))
    own = pltpu.make_async_copy(pts.at[part_at(r), :], cols.at[part_at(t), :], local_sem)
    own.start()
    pl.semaphore_wait(barrier, chips + reps - 1)

    def points_copy(owner, target):
        return remote(
            pts.at[part_at(r), :], cols.at[part_at(owner), :],
            send_sem.at[0], rv_pts.at[owner], {"team": target},
        )

    def forward_copy(owner):
        return remote(
            cols.at[part_at(owner), :], cols.at[part_at(owner), :],
            send_sem.at[1], rv_fwd.at[owner], {"team": sibling},
        )

    def send_points(i, carry):
        for h in range(2):
            q = 4 * chunk_of(i) + 2 * h + core

            @pl.when(q != t)
            def _():
                points_copy(t, q).start()

        return carry

    lax.fori_loop(0, chunks, send_points, 0)
    pend.append(lambda: each(1, chips, lambda k: points_copy(t, t).wait_send()))
    own.wait()

    def widen_rows(b, carry):
        block = pts[block_at(b), :]
        rows_aug[block_at(b), pl.ds(0, LANES)] = block
        rows_aug[block_at(b), pl.ds(LANES, LANES)] = extra_lanes(block, 0, 3)
        return carry

    lax.fori_loop(0, blocks, widen_rows, 0)

    def relay_chunk(i):
        for h in range(2):
            q = 4 * chunk_of(i) + 2 * h + core

            @pl.when(q != t)
            def _():
                points_copy(q, q).wait_recv()

            forward_copy(q).start()

    pend.append(lambda: each(0, chips, lambda k: forward_copy(t).wait_send()))

    def sib_copy(c, src):
        return remote(
            part_one.at[src], sib_one.at[c], send_sem.at[2], rv_sib.at[c], {"team": sibling}
        )

    def first_chunk(i, carry):
        c = chunk_of(i)

        @pl.when(i + 1 < chunks)
        def _():
            relay_chunk(i + 1)

        for h in range(2):
            forward_copy(4 * c + 2 * h + 1 - core).wait_recv()
        block = cols[chunk_at(c), :]
        extra = extra_lanes(block, 3, 0)
        wide = jnp.concatenate([block, extra], axis=1)
        acc = jnp.zeros((1, 256), jnp.float32)
        for b in range(max(rows // 256, 1)):
            size = min(rows, 256)
            tile = lax.dot_general(
                rows_aug[pl.ds(b * size, size), :], wide, nt, preferred_element_type=jnp.float32
            )
            tile = tile * (0.5 * LOG2E)
            expo[pl.ds(b * size, size), chunk_at(c)] = tile
            acc = acc + jnp.sum(jnp.exp2(0.5 * tile), axis=0, keepdims=True)
        part_one[2 * c] = acc[:, :LANES]
        part_one[2 * c + 1] = acc[:, LANES:]
        sib_copy(c, 2 * c + 1 - core).start()
        return carry

    relay_chunk(0)
    lax.fori_loop(0, chunks, first_chunk, 0)
    pend.append(lambda: each(0, chunks, lambda c: sib_copy(c, 2 * c).wait_send()))

    def add_sibling(c, carry):
        sib_copy(c, 2 * c).wait_recv()
        chip_one[pl.ds(c, 1), :] = part_one[2 * c + core] + sib_one[c]
        return carry

    lax.fori_loop(0, chunks, add_sibling, 0)

    def one_copy(owner, target):
        return remote(
            chip_one, got_one.at[owner], send_sem.at[3], rv_one.at[owner], {"team": target}
        )

    each(1, chips, lambda k: one_copy(t // 2, same_core(k)).start())
    pend.append(lambda: each(1, chips, lambda k: one_copy(0, t).wait_send()))
    got_one[t // 2] = chip_one[...]
    each(1, chips, lambda k: one_copy(same_core(k) // 2, t).wait_recv())
    first = got_one[0]
    for q in range(1, chips):
        first = first + got_one[q]
    pot[core] = -2.0 * (jnp.log(first) - log_count)

    def pot_copy(owner):
        return remote(
            pot.at[owner], pot.at[owner], send_sem.at[4], rv_pot, {"team": sibling}
        )

    pot_copy(core).start()
    pend.append(lambda: pot_copy(core).wait_send())
    pot_copy(1 - core).wait_recv()
    pot_scaled[...] = pot[...] * (0.5 * LOG2E)

    def second_block(b):
        acc = jnp.zeros((LANES, LANES), jnp.float32)
        total = jnp.zeros((LANES, LANES), jnp.float32)
        for s in range(chunks):
            tile = expo[block_at(b), pl.ds(s * 256, 256)]
            left = jnp.exp2(tile[:, :LANES] + pot_scaled[0, s : s + 1, :])
            right = jnp.exp2(tile[:, LANES:] + pot_scaled[1, s : s + 1, :])
            acc = acc + left + right
            rounded = jnp.concatenate(
                [left.astype(jnp.bfloat16), right.astype(jnp.bfloat16)], axis=1
            )
            total = total + jnp.dot(
                rounded, cols[pl.ds(s * 256, 256), :], preferred_element_type=jnp.float32
            )
        return row_of(acc), total

    def xnum_copy(b, slot):
        return remote(
            numer.at[block_at(b), :], far_numer.at[slot],
            send_sem.at[5], rv_xnum.at[slot], {"rep": across},
        )

    def xtwo_copy(b, slot):
        return remote(
            sum_two.at[b], far_two.at[slot],
            send_sem.at[6], rv_xtwo.at[slot], {"rep": across},
        )

    def turn(i):
        return lax.rem(z // 2 + 1 + i, half_blocks)

    def far_block(i, carry):
        slot = turn(i)
        b = (1 - near) * half_blocks + slot
        row, total = second_block(b)
        numer[block_at(b), :] = total
        sum_two[b] = row
        xnum_copy(b, slot).start()
        xtwo_copy(b, slot).start()
        return carry

    lax.fori_loop(0, half_blocks, far_block, 0)
    pend.append(lambda: each(0, half_blocks, lambda k: xnum_copy(k, k).wait_send()))
    pend.append(lambda: each(0, half_blocks, lambda k: xtwo_copy(k, k).wait_send()))

    def num_copy(dest, owner):
        return remote(
            numer.at[part_at(dest), :], got_numer.at[owner],
            send_sem.at[7], rv_num.at[owner], {"rep": dest},
        )

    def two_copy(b, dest, owner):
        return remote(
            sum_two.at[b], got_two.at[owner],
            send_sem.at[8], rv_two.at[owner], {"rep": dest},
        )

    def near_block(i, carry):
        slot = turn(i)
        b = near * half_blocks + slot
        row, total = second_block(b)
        xnum_copy(b, slot).wait_recv()
        xtwo_copy(b, slot).wait_recv()
        numer[block_at(b), :] = total + far_numer[slot]
        sum_two[b] = row + far_two[slot]
        for h in range(2):
            q = 2 * b + h

            @pl.when(q != r)
            def _():
                two_copy(b, q, z).start()
                num_copy(q, z).start()

        return carry

    lax.fori_loop(0, half_blocks, near_block, 0)
    pend.append(lambda: each(1, depth, lambda k: num_copy(r, z).wait_send()))
    pend.append(lambda: each(1, depth, lambda k: two_copy(0, r, z).wait_send()))
    got_two[z] = sum_two[r // 2]
    got_numer[z] = numer[part_at(r), :]
    each(1, depth, lambda k: two_copy(0, r, lax.rem(z + k, depth)).wait_recv())
    second = got_two[0]
    for q in range(1, depth):
        second = second + got_two[q]
    half = lax.rem(r, 2)
    pot_own = pot[lax.rem(t // 2, 2), pl.ds(home, 1), :]
    pot_own = jnp.where(half == core, pot_own, pltpu.roll(pot_own, PART, 1))
    pot_all[r] = 0.5 * (pot_own - 2.0 * (jnp.log(second) - log_count))

    def fin_copy(owner, target):
        return remote(
            pot_all.at[owner], pot_all.at[owner],
            send_sem.at[9], rv_fin.at[owner], {"rep": target},
        )

    each(1, reps, lambda k: fin_copy(r, rep_peer(k)).start())
    pend.append(lambda: each(1, reps, lambda k: fin_copy(r, r).wait_send()))
    lane = lax.broadcasted_iota(jnp.int32, (PART, LANES), 1)
    sub = lax.broadcasted_iota(jnp.int32, (PART, LANES), 0)
    divisor = jnp.sum(jnp.where(lane == sub + half * PART, second, 0.0), axis=1, keepdims=True)
    each(1, depth, lambda k: num_copy(r, lax.rem(z + k, depth)).wait_recv())
    weighted = got_numer[0]
    for q in range(1, depth):
        weighted = weighted + got_numer[q]
    disp_mine[...] = pts[part_at(r), :].astype(jnp.float32) - weighted / divisor

    def disp_copy(owner, target):
        return remote(
            disp_mine, disp_out.at[part_at(owner), :],
            send_sem.at[10], rv_disp.at[owner], {"rep": target},
        )

    def side_copy(owner, src):
        return remote(
            src, disp_out.at[part_at(owner), :],
            send_sem.at[11], rv_side.at[owner], {"rep": across},
        )

    side_copy(r, disp_mine).start()
    each(1, depth, lambda k: disp_copy(r, z_peer(k)).start())
    pend.append(lambda: each(1, depth, lambda k: disp_copy(r, r).wait_send()))
    pend.append(lambda: each(0, depth, lambda k: side_copy(r, disp_mine).wait_send()))
    keep = pltpu.make_async_copy(disp_mine, disp_out.at[part_at(r), :], local_sem)
    keep.start()

    def pass_on(k):
        q = z_peer(k)
        disp_copy(q, r).wait_recv()
        side_copy(q, disp_out.at[part_at(q), :]).start()

    each(1, depth, pass_on)
    each(1, reps, lambda k: fin_copy(rep_peer(k), r).wait_recv())
    low_lane = lax.broadcasted_iota(jnp.int32, (1, LANES), 1) < PART
    for b in range(blocks):
        pot_out[b] = jnp.where(low_lane, pot_all[2 * b], pot_all[2 * b + 1])
    finish()
    each(0, depth, lambda k: side_copy(lax.rem(z_peer(k) + depth, reps), disp_mine).wait_recv())
    keep.wait()


def shards(points):
    rows, width = points.shape
    teams = lax.axis_size("team")
    reps = lax.axis_size("rep")
    blocks = rows // LANES
    chunks = teams * PART // 256
    depth = reps // 2
    f32 = jnp.float32
    dma = pltpu.SemaphoreType.DMA
    vmem = pltpu.VMEM
    potential, displacement = pl.pallas_call(
        functools.partial(body, teams, reps),
        out_shape=(
            jax.ShapeDtypeStruct((blocks, 1, LANES), f32),
            jax.ShapeDtypeStruct((rows, width), f32),
        ),
        in_specs=[pl.BlockSpec(memory_space=pltpu.VMEM)],
        out_specs=(
            pl.BlockSpec(memory_space=pltpu.VMEM),
            pl.BlockSpec(memory_space=pl.ANY),
        ),
        scratch_shapes=[
            vmem((rows, 2 * width), jnp.bfloat16),
            vmem((teams * PART, width), jnp.bfloat16),
            vmem((rows, teams * PART), f32),
            vmem((2 * chunks, 1, LANES), f32),
            vmem((chunks, 1, LANES), f32),
            vmem((chunks, LANES), f32),
            vmem((teams // 2, chunks, LANES), f32),
            vmem((2, chunks, LANES), f32),
            vmem((2, chunks, LANES), f32),
            vmem((rows, width), f32),
            vmem((blocks, 1, LANES), f32),
            vmem((blocks // 2, LANES, width), f32),
            vmem((blocks // 2, 1, LANES), f32),
            vmem((depth, PART, width), f32),
            vmem((depth, 1, LANES), f32),
            vmem((PART, width), f32),
            vmem((reps, 1, LANES), f32),
            dma((12,)),
            dma,
            dma((teams,)),
            dma((teams,)),
            dma((chunks,)),
            dma((teams // 2,)),
            dma,
            dma((blocks // 2,)),
            dma((blocks // 2,)),
            dma((depth,)),
            dma((depth,)),
            dma((reps,)),
            dma((reps,)),
            dma((reps,)),
        ],
        compiler_params=pltpu.CompilerParams(collective_id=0, has_side_effects=True),
    )(points)
    return potential.reshape(rows), displacement


def solution(mesh):
    return jax.shard_map(
        shards,
        mesh=mesh,
        in_specs=(P("team", None),),
        out_specs=(P("team"), P("team", None)),
        check_vma=False,
    )
```

```python
import functools
import math

import jax
import jax.numpy as jnp
from jax import lax
from jax.experimental import pallas as pl
from jax.experimental.pallas import tpu as pltpu
from jax.sharding import PartitionSpec as P

LANES = 128
PART = 64
LEAD = 2
MESH = pl.DeviceIdType.MESH
LOG2E = math.log2(math.e)


def split3(value):
    high = value.astype(jnp.bfloat16).astype(jnp.float32)
    rest = value - high
    mid = rest.astype(jnp.bfloat16).astype(jnp.float32)
    return high, mid, rest - mid


def extra_lanes(block, first, ones):
    wide = block.astype(jnp.float32)
    half = -0.5 * jnp.sum(wide * wide, axis=1, keepdims=True)
    high, mid, low = split3(half)
    lane = lax.broadcasted_iota(jnp.int32, wide.shape, 1)
    extra = jnp.where((lane >= ones) & (lane < ones + 3), 1.0, 0.0)
    extra = jnp.where(lane == first, high, extra)
    extra = jnp.where(lane == first + 1, mid, extra)
    extra = jnp.where(lane == first + 2, low, extra)
    return extra.astype(jnp.bfloat16)


def row_of(acc):
    size = acc.shape[0]
    total = jnp.sum(acc, axis=1, keepdims=True)
    lane = lax.broadcasted_iota(jnp.int32, (size, LANES), 1)
    sub = lax.broadcasted_iota(jnp.int32, (size, LANES), 0)
    return jnp.sum(jnp.where(lane == sub, total, 0.0), axis=0, keepdims=True)


def body(
    teams, reps, pts, pot_out, disp_out,
    mate, rows_aug, cols, expo, chip_one, got_one, pot, pot_scaled,
    out_numer, out_two, sib_numer, sib_two,
    numer, sum_two, far_numer, far_two, got_numer, got_two, disp_mine, pot_all,
    send_sem, local_sem, rv_mate, rv_pts, rv_one, rv_snum, rv_stwo,
    rv_xnum, rv_xtwo, rv_num, rv_two, rv_disp, rv_side, rv_fin,
):
    rows = pts.shape[0]
    blocks = rows // LANES
    chips = teams // 2
    chunks = chips // 2
    depth = reps // 2
    half_blocks = blocks // 2
    log_count = math.log(rows * teams)
    t = lax.axis_index("team")
    r = lax.axis_index("rep")
    core = lax.rem(t, 2)
    sibling = t + 1 - 2 * core
    near = r // depth
    z = lax.rem(r, depth)
    across = lax.rem(r + depth, reps)
    pairs = chunks // 2
    home = t // 4
    nt = (((1,), (1,)), ((), ()))

    def part_at(index):
        return pl.ds(pl.multiple_of(index * PART, PART), PART)

    def block_at(index):
        return pl.ds(pl.multiple_of(index * LANES, LANES), LANES)

    def remote(src, dst, send, recv, where):
        return pltpu.make_async_remote_copy(
            src_ref=src, dst_ref=dst, send_sem=send, recv_sem=recv,
            device_id=where, device_id_type=MESH,
        )

    def each(first, count, step):
        lax.fori_loop(first, count, lambda k, c: (step(k), c)[1], 0)

    def same_core(k):
        return lax.rem(t + 2 * k, teams)

    def rep_peer(k):
        return lax.rem(r + k, reps)

    def z_peer(k):
        return near * depth + lax.rem(z + k, depth)

    def chunk_of(i):
        side, step = lax.rem(i, 2), i // 2
        step = step + (step // 2) * (1 - 2 * lax.rem(step, 2))
        return lax.rem(home // pairs + side, 2) * pairs + lax.rem(home + step, pairs)

    pend = []

    def finish():
        for step in pend:
            step()

    barrier = pltpu.get_barrier_semaphore()

    def greet(where):
        pl.semaphore_signal(barrier, 1, device_id=where, device_id_type=MESH)

    each(1, chips, lambda k: greet({"team": same_core(k)}))
    greet({"team": sibling})
    each(1, reps, lambda k: greet({"rep": rep_peer(k)}))
    own = pltpu.make_async_copy(pts.at[part_at(r), :], cols.at[part_at(t // 2), :], local_sem)
    own.start()
    pl.semaphore_wait(barrier, chips + reps - 1)

    def points_copy(owner, target):
        return remote(
            pts.at[part_at(r), :], cols.at[part_at(owner), :],
            send_sem.at[0], rv_pts.at[owner], {"team": target},
        )

    def send_points(i, carry):
        for h in range(2):
            q = 4 * chunk_of(i) + 2 * h + core

            @pl.when(q != t)
            def _():
                points_copy(t // 2, q).start()

        return carry

    lax.fori_loop(0, chunks, send_points, 0)
    pend.append(lambda: each(1, chips, lambda k: points_copy(t // 2, t).wait_send()))
    mate_copy = remote(pts, mate, send_sem.at[1], rv_mate, {"team": sibling})
    mate_copy.start()
    pend.append(mate_copy.wait_send)
    own.wait()

    def widen_from(ref, first):
        def widen_rows(b, carry):
            block = ref[block_at(b), :]
            rows_aug[block_at(first + b), pl.ds(0, LANES)] = block
            rows_aug[block_at(first + b), pl.ds(LANES, LANES)] = extra_lanes(block, 0, 3)
            return carry

        lax.fori_loop(0, blocks, widen_rows, 0)

    widen_from(pts, 0)
    mate_copy.wait_recv()
    widen_from(mate, blocks)

    def first_chunk(i, carry):
        c = chunk_of(i)
        for h in range(2):
            k = 2 * c + h

            @pl.when(k != t // 2)
            def _():
                points_copy(k, t).wait_recv()

        block = cols[block_at(c), :]
        wide = jnp.concatenate([block, extra_lanes(block, 3, 0)], axis=1)
        acc = jnp.zeros((1, LANES), jnp.float32)
        for b in range(2 * rows // 256):
            tile = lax.dot_general(
                rows_aug[pl.ds(b * 256, 256), :], wide, nt, preferred_element_type=jnp.float32
            )
            tile = tile * (0.5 * LOG2E)
            expo[c, pl.ds(b * 256, 256), :] = tile
            acc = acc + jnp.sum(jnp.exp2(0.5 * tile), axis=0, keepdims=True)
        chip_one[pl.ds(c, 1), :] = acc
        return carry

    lax.fori_loop(0, chunks, first_chunk, 0)

    def one_copy(owner, target):
        return remote(
            chip_one, got_one.at[owner], send_sem.at[3], rv_one.at[owner], {"team": target}
        )

    each(1, chips, lambda k: one_copy(t // 2, same_core(k)).start())
    pend.append(lambda: each(1, chips, lambda k: one_copy(0, t).wait_send()))
    got_one[t // 2] = chip_one[...]
    each(1, chips, lambda k: one_copy(same_core(k) // 2, t).wait_recv())
    first = got_one[0]
    for q in range(1, chips):
        first = first + got_one[q]
    pot[...] = -2.0 * (jnp.log(first) - log_count)

    pot_scaled[...] = pot[...] * (0.5 * LOG2E)

    def second_block(b):
        acc = jnp.zeros((LANES, LANES), jnp.float32)
        total = jnp.zeros((LANES, LANES), jnp.float32)
        for s in range(chunks // 2):
            left = jnp.exp2(expo[2 * s, block_at(b), :] + pot_scaled[2 * s : 2 * s + 1, :])
            right = jnp.exp2(expo[2 * s + 1, block_at(b), :] + pot_scaled[2 * s + 1 : 2 * s + 2, :])
            acc = acc + left + right
            rounded = jnp.concatenate(
                [left.astype(jnp.bfloat16), right.astype(jnp.bfloat16)], axis=1
            )
            total = total + jnp.dot(
                rounded, cols[pl.ds(s * 256, 256), :], preferred_element_type=jnp.float32
            )
        return row_of(acc), total

    def snum_copy(b):
        return remote(
            out_numer.at[b], sib_numer.at[b], send_sem.at[2], rv_snum.at[b], {"team": sibling}
        )

    def stwo_copy(b):
        return remote(
            out_two.at[b], sib_two.at[b], send_sem.at[4], rv_stwo.at[b], {"team": sibling}
        )

    def xnum_copy(b, slot):
        return remote(
            numer.at[block_at(b), :], far_numer.at[slot],
            send_sem.at[5], rv_xnum.at[slot], {"rep": across},
        )

    def xtwo_copy(b, slot):
        return remote(
            sum_two.at[b], far_two.at[slot],
            send_sem.at[6], rv_xtwo.at[slot], {"rep": across},
        )

    def turn(i):
        return lax.rem(z // 2 + 1 + i, half_blocks)

    def num_copy(dest, owner):
        return remote(
            numer.at[part_at(dest), :], got_numer.at[owner],
            send_sem.at[7], rv_num.at[owner], {"rep": dest},
        )

    def two_copy(b, dest, owner):
        return remote(
            sum_two.at[b], got_two.at[owner],
            send_sem.at[8], rv_two.at[owner], {"rep": dest},
        )

    def place(i):
        side, slot = i // half_blocks, turn(lax.rem(i, half_blocks))
        return side, slot, lax.rem(1 - near + side, 2) * half_blocks + slot

    def for_sibling(i):
        b = place(i)[2]
        row, total = second_block(blocks + b)
        out_numer[b] = total
        out_two[b] = row
        snum_copy(b).start()
        stwo_copy(b).start()

    def for_own(i):
        side, slot, b = place(i)
        row, total = second_block(b)
        snum_copy(b).wait_recv()
        stwo_copy(b).wait_recv()
        numer[block_at(b), :] = total + sib_numer[b]
        sum_two[b] = row + sib_two[b]

        @pl.when(side == 0)
        def _():
            xnum_copy(b, slot).start()
            xtwo_copy(b, slot).start()

        @pl.when(side == 1)
        def _():
            xnum_copy(b, slot).wait_recv()
            xtwo_copy(b, slot).wait_recv()
            numer[block_at(b), :] = numer[block_at(b), :] + far_numer[slot]
            sum_two[b] = sum_two[b] + far_two[slot]
            for h in range(2):
                q = 2 * b + h

                @pl.when(q != r)
                def _():
                    two_copy(b, q, z).start()
                    num_copy(q, z).start()

    def second_step(i, carry):
        @pl.when(i < blocks)
        def _():
            for_sibling(i)

        @pl.when(i >= LEAD)
        def _():
            for_own(i - LEAD)

        return carry

    lax.fori_loop(0, blocks + LEAD, second_step, 0)
    pend.append(lambda: each(0, blocks, lambda k: snum_copy(k).wait_send()))
    pend.append(lambda: each(0, blocks, lambda k: stwo_copy(k).wait_send()))
    pend.append(lambda: each(0, half_blocks, lambda k: xnum_copy(k, k).wait_send()))
    pend.append(lambda: each(0, half_blocks, lambda k: xtwo_copy(k, k).wait_send()))
    pend.append(lambda: each(1, depth, lambda k: num_copy(r, z).wait_send()))
    pend.append(lambda: each(1, depth, lambda k: two_copy(0, r, z).wait_send()))
    got_two[z] = sum_two[r // 2]
    got_numer[z] = numer[part_at(r), :]
    each(1, depth, lambda k: two_copy(0, r, lax.rem(z + k, depth)).wait_recv())
    second = got_two[0]
    for q in range(1, depth):
        second = second + got_two[q]
    half = lax.rem(r, 2)
    pot_own = pot[pl.ds(home, 1), :]
    pot_own = jnp.where(half == lax.rem(t // 2, 2), pot_own, pltpu.roll(pot_own, PART, 1))
    pot_all[r] = 0.5 * (pot_own - 2.0 * (jnp.log(second) - log_count))

    def fin_copy(owner, target):
        return remote(
            pot_all.at[owner], pot_all.at[owner],
            send_sem.at[9], rv_fin.at[owner], {"rep": target},
        )

    each(1, reps, lambda k: fin_copy(r, rep_peer(k)).start())
    pend.append(lambda: each(1, reps, lambda k: fin_copy(r, r).wait_send()))
    lane = lax.broadcasted_iota(jnp.int32, (PART, LANES), 1)
    sub = lax.broadcasted_iota(jnp.int32, (PART, LANES), 0)
    divisor = jnp.sum(jnp.where(lane == sub + half * PART, second, 0.0), axis=1, keepdims=True)
    each(1, depth, lambda k: num_copy(r, lax.rem(z + k, depth)).wait_recv())
    weighted = got_numer[0]
    for q in range(1, depth):
        weighted = weighted + got_numer[q]
    disp_mine[...] = pts[part_at(r), :].astype(jnp.float32) - weighted / divisor

    def disp_copy(owner, target):
        return remote(
            disp_mine, disp_out.at[part_at(owner), :],
            send_sem.at[10], rv_disp.at[owner], {"rep": target},
        )

    def side_copy(owner, src, target):
        return remote(
            src, disp_out.at[part_at(owner), :],
            send_sem.at[11], rv_side.at[owner], {"rep": target},
        )

    opposite = lax.rem(z_peer(depth // 2) + depth, reps)
    side_copy(r, disp_mine, opposite).start()
    side_copy(r, disp_mine, across).start()
    each(1, depth, lambda k: disp_copy(r, z_peer(k)).start())
    pend.append(lambda: each(1, depth, lambda k: disp_copy(r, r).wait_send()))
    pend.append(lambda: each(0, depth, lambda k: side_copy(r, disp_mine, across).wait_send()))
    keep = pltpu.make_async_copy(disp_mine, disp_out.at[part_at(r), :], local_sem)
    keep.start()

    def pass_on(k):
        q = z_peer(k)
        disp_copy(q, r).wait_recv()

        @pl.when(k != depth // 2)
        def _():
            side_copy(q, disp_out.at[part_at(q), :], across).start()

    each(1, depth, pass_on)
    each(1, reps, lambda k: fin_copy(rep_peer(k), r).wait_recv())
    low_lane = lax.broadcasted_iota(jnp.int32, (1, LANES), 1) < PART
    for b in range(blocks):
        pot_out[b] = jnp.where(low_lane, pot_all[2 * b], pot_all[2 * b + 1])
    finish()
    each(0, depth, lambda k: side_copy(lax.rem(z_peer(k) + depth, reps), disp_mine, r).wait_recv())
    keep.wait()


def shards(points):
    rows, width = points.shape
    teams = lax.axis_size("team")
    reps = lax.axis_size("rep")
    blocks = rows // LANES
    chips = teams // 2
    chunks = chips // 2
    depth = reps // 2
    f32 = jnp.float32
    dma = pltpu.SemaphoreType.DMA
    vmem = pltpu.VMEM
    potential, displacement = pl.pallas_call(
        functools.partial(body, teams, reps),
        out_shape=(
            jax.ShapeDtypeStruct((blocks, 1, LANES), f32),
            jax.ShapeDtypeStruct((rows, width), f32),
        ),
        in_specs=[pl.BlockSpec(memory_space=pltpu.VMEM)],
        out_specs=(
            pl.BlockSpec(memory_space=pltpu.VMEM),
            pl.BlockSpec(memory_space=pl.ANY),
        ),
        scratch_shapes=[
            vmem((rows, width), jnp.bfloat16),
            vmem((2 * rows, 2 * width), jnp.bfloat16),
            vmem((chips * PART, width), jnp.bfloat16),
            vmem((chunks, 2 * rows, LANES), f32),
            vmem((chunks, LANES), f32),
            vmem((chips, chunks, LANES), f32),
            vmem((chunks, LANES), f32),
            vmem((chunks, LANES), f32),
            vmem((blocks, LANES, width), f32),
            vmem((blocks, 1, LANES), f32),
            vmem((blocks, LANES, width), f32),
            vmem((blocks, 1, LANES), f32),
            vmem((rows, width), f32),
            vmem((blocks, 1, LANES), f32),
            vmem((blocks // 2, LANES, width), f32),
            vmem((blocks // 2, 1, LANES), f32),
            vmem((depth, PART, width), f32),
            vmem((depth, 1, LANES), f32),
            vmem((PART, width), f32),
            vmem((reps, 1, LANES), f32),
            dma((12,)),
            dma,
            dma,
            dma((chips,)),
            dma((chips,)),
            dma((blocks,)),
            dma((blocks,)),
            dma((blocks // 2,)),
            dma((blocks // 2,)),
            dma((depth,)),
            dma((depth,)),
            dma((reps,)),
            dma((reps,)),
            dma((reps,)),
        ],
        compiler_params=pltpu.CompilerParams(collective_id=0, has_side_effects=True),
    )(points)
    return potential.reshape(rows), displacement


def solution(mesh):
    return jax.shard_map(
        shards,
        mesh=mesh,
        in_specs=(P("team", None),),
        out_specs=(P("team"), P("team", None)),
        check_vma=False,
    )
```

```python
import functools
import math

import jax
import jax.numpy as jnp
from jax import lax
from jax.experimental import pallas as pl
from jax.experimental.pallas import tpu as pltpu
from jax.sharding import PartitionSpec as P

LANES = 128
PART = 64
LEAD = 2
MESH = pl.DeviceIdType.MESH
LOG2E = math.log2(math.e)


SCALE = 8192.0


def encode(value):
    power = value * SCALE
    for _ in range(3):
        power = power * power
    return jnp.where(value < 0.0, -power, power).astype(jnp.bfloat16)


def decode(code):
    power = code.astype(jnp.float32)
    size = jnp.sqrt(jnp.sqrt(jnp.sqrt(jnp.abs(power)))) * (1.0 / SCALE)
    return jnp.where(power < 0.0, -size, size)


def split3(value):
    high = value.astype(jnp.bfloat16).astype(jnp.float32)
    rest = value - high
    mid = rest.astype(jnp.bfloat16).astype(jnp.float32)
    return high, mid, rest - mid


def extra_lanes(block, first, ones):
    wide = block.astype(jnp.float32)
    half = -0.5 * jnp.sum(wide * wide, axis=1, keepdims=True)
    high, mid, low = split3(half)
    lane = lax.broadcasted_iota(jnp.int32, wide.shape, 1)
    extra = jnp.where((lane >= ones) & (lane < ones + 3), 1.0, 0.0)
    extra = jnp.where(lane == first, high, extra)
    extra = jnp.where(lane == first + 1, mid, extra)
    extra = jnp.where(lane == first + 2, low, extra)
    return extra.astype(jnp.bfloat16)


def row_of(acc):
    size = acc.shape[0]
    total = jnp.sum(acc, axis=1, keepdims=True)
    lane = lax.broadcasted_iota(jnp.int32, (size, LANES), 1)
    sub = lax.broadcasted_iota(jnp.int32, (size, LANES), 0)
    return jnp.sum(jnp.where(lane == sub, total, 0.0), axis=0, keepdims=True)


def body(
    teams, reps, pts, pot_out, disp_out,
    mate, rows_aug, cols, expo, chip_one, got_one, pot, pot_scaled,
    out_numer, out_two, sib_numer, sib_two,
    numer, sum_two, far_numer, far_two, got_numer, got_two, disp_mine, pot_all,
    send_sem, local_sem, rv_mate, rv_pts, rv_one, rv_snum, rv_stwo,
    rv_xnum, rv_xtwo, rv_num, rv_two, rv_disp, rv_fin,
):
    rows = pts.shape[0]
    blocks = rows // LANES
    chips = teams // 2
    chunks = chips // 2
    depth = reps // 2
    half_blocks = blocks // 2
    log_count = math.log(rows * teams)
    t = lax.axis_index("team")
    r = lax.axis_index("rep")
    core = lax.rem(t, 2)
    sibling = t + 1 - 2 * core
    near = r // depth
    z = lax.rem(r, depth)
    across = lax.rem(r + depth, reps)
    pairs = chunks // 2
    home = t // 4
    nt = (((1,), (1,)), ((), ()))

    def part_at(index):
        return pl.ds(pl.multiple_of(index * PART, PART), PART)

    def block_at(index):
        return pl.ds(pl.multiple_of(index * LANES, LANES), LANES)

    def remote(src, dst, send, recv, where):
        return pltpu.make_async_remote_copy(
            src_ref=src, dst_ref=dst, send_sem=send, recv_sem=recv,
            device_id=where, device_id_type=MESH,
        )

    def each(first, count, step):
        lax.fori_loop(first, count, lambda k, c: (step(k), c)[1], 0)

    def same_core(k):
        return lax.rem(t + 2 * k, teams)

    def rep_peer(k):
        return lax.rem(r + k, reps)

    def z_peer(k):
        return near * depth + lax.rem(z + k, depth)

    def chunk_of(i):
        side, step = lax.rem(i, 2), i // 2
        step = step + (step // 2) * (1 - 2 * lax.rem(step, 2))
        return lax.rem(home // pairs + side, 2) * pairs + lax.rem(home + step, pairs)

    pend = []

    def finish():
        for step in pend:
            step()

    barrier = pltpu.get_barrier_semaphore()

    def greet(where):
        pl.semaphore_signal(barrier, 1, device_id=where, device_id_type=MESH)

    each(1, chips, lambda k: greet({"team": same_core(k)}))
    greet({"team": sibling})
    each(1, reps, lambda k: greet({"rep": rep_peer(k)}))
    own = pltpu.make_async_copy(pts.at[part_at(r), :], cols.at[part_at(t // 2), :], local_sem)
    own.start()
    pl.semaphore_wait(barrier, chips + reps - 1)

    def points_copy(owner, target):
        return remote(
            pts.at[part_at(r), :], cols.at[part_at(owner), :],
            send_sem.at[0], rv_pts.at[owner], {"team": target},
        )

    def send_points(i, carry):
        for h in range(2):
            q = 4 * chunk_of(i) + 2 * h + core

            @pl.when(q != t)
            def _():
                points_copy(t // 2, q).start()

        return carry

    lax.fori_loop(0, chunks, send_points, 0)
    pend.append(lambda: each(1, chips, lambda k: points_copy(t // 2, t).wait_send()))
    mate_copy = remote(pts, mate, send_sem.at[1], rv_mate, {"team": sibling})
    mate_copy.start()
    pend.append(mate_copy.wait_send)
    own.wait()

    def widen_from(ref, first):
        def widen_rows(b, carry):
            block = ref[block_at(b), :]
            rows_aug[block_at(first + b), pl.ds(0, LANES)] = block
            rows_aug[block_at(first + b), pl.ds(LANES, LANES)] = extra_lanes(block, 0, 3)
            return carry

        lax.fori_loop(0, blocks, widen_rows, 0)

    widen_from(pts, 0)
    mate_copy.wait_recv()
    widen_from(mate, blocks)

    def first_chunk(i, carry):
        c = chunk_of(i)
        for h in range(2):
            k = 2 * c + h

            @pl.when(k != t // 2)
            def _():
                points_copy(k, t).wait_recv()

        block = cols[block_at(c), :]
        wide = jnp.concatenate([block, extra_lanes(block, 3, 0)], axis=1)
        acc = jnp.zeros((1, LANES), jnp.float32)
        for b in range(2 * rows // 256):
            tile = lax.dot_general(
                rows_aug[pl.ds(b * 256, 256), :], wide, nt, preferred_element_type=jnp.float32
            )
            tile = tile * (0.5 * LOG2E)
            expo[c, pl.ds(b * 256, 256), :] = tile
            acc = acc + jnp.sum(jnp.exp2(0.5 * tile), axis=0, keepdims=True)
        chip_one[pl.ds(c, 1), :] = acc
        return carry

    lax.fori_loop(0, chunks, first_chunk, 0)

    def one_copy(owner, target):
        return remote(
            chip_one, got_one.at[owner], send_sem.at[3], rv_one.at[owner], {"team": target}
        )

    each(1, chips, lambda k: one_copy(t // 2, same_core(k)).start())
    pend.append(lambda: each(1, chips, lambda k: one_copy(0, t).wait_send()))
    got_one[t // 2] = chip_one[...]
    each(1, chips, lambda k: one_copy(same_core(k) // 2, t).wait_recv())
    first = got_one[0]
    for q in range(1, chips):
        first = first + got_one[q]
    pot[...] = -2.0 * (jnp.log(first) - log_count)

    pot_scaled[...] = pot[...] * (0.5 * LOG2E)

    def second_block(b):
        acc = jnp.zeros((LANES, LANES), jnp.float32)
        total = jnp.zeros((LANES, LANES), jnp.float32)
        for s in range(chunks // 2):
            left = jnp.exp2(expo[2 * s, block_at(b), :] + pot_scaled[2 * s : 2 * s + 1, :])
            right = jnp.exp2(expo[2 * s + 1, block_at(b), :] + pot_scaled[2 * s + 1 : 2 * s + 2, :])
            acc = acc + left + right
            rounded = jnp.concatenate(
                [left.astype(jnp.bfloat16), right.astype(jnp.bfloat16)], axis=1
            )
            total = total + jnp.dot(
                rounded, cols[pl.ds(s * 256, 256), :], preferred_element_type=jnp.float32
            )
        return row_of(acc), total

    def snum_copy(b):
        return remote(
            out_numer.at[b], sib_numer.at[b], send_sem.at[2], rv_snum.at[b], {"team": sibling}
        )

    def stwo_copy(b):
        return remote(
            out_two.at[b], sib_two.at[b], send_sem.at[4], rv_stwo.at[b], {"team": sibling}
        )

    def xnum_copy(b, slot):
        return remote(
            numer.at[block_at(b), :], far_numer.at[slot],
            send_sem.at[5], rv_xnum.at[slot], {"rep": across},
        )

    def xtwo_copy(b, slot):
        return remote(
            sum_two.at[b], far_two.at[slot],
            send_sem.at[6], rv_xtwo.at[slot], {"rep": across},
        )

    def turn(i):
        return lax.rem(z // 2 + 1 + i, half_blocks)

    def num_copy(dest, owner):
        return remote(
            numer.at[part_at(dest), :], got_numer.at[owner],
            send_sem.at[7], rv_num.at[owner], {"rep": dest},
        )

    def two_copy(b, dest, owner):
        return remote(
            sum_two.at[b], got_two.at[owner],
            send_sem.at[8], rv_two.at[owner], {"rep": dest},
        )

    def place(i):
        side, slot = i // half_blocks, turn(lax.rem(i, half_blocks))
        return side, slot, lax.rem(1 - near + side, 2) * half_blocks + slot

    def for_sibling(i):
        b = place(i)[2]
        row, total = second_block(blocks + b)
        out_numer[b] = total
        out_two[b] = row
        snum_copy(b).start()
        stwo_copy(b).start()

    def for_own(i):
        side, slot, b = place(i)
        row, total = second_block(b)
        snum_copy(b).wait_recv()
        stwo_copy(b).wait_recv()
        numer[block_at(b), :] = total + sib_numer[b]
        sum_two[b] = row + sib_two[b]

        @pl.when(side == 0)
        def _():
            xnum_copy(b, slot).start()
            xtwo_copy(b, slot).start()

        @pl.when(side == 1)
        def _():
            xnum_copy(b, slot).wait_recv()
            xtwo_copy(b, slot).wait_recv()
            numer[block_at(b), :] = numer[block_at(b), :] + far_numer[slot]
            sum_two[b] = sum_two[b] + far_two[slot]
            for h in range(2):
                q = 2 * b + h

                @pl.when(q != r)
                def _():
                    two_copy(b, q, z).start()
                    num_copy(q, z).start()

    def second_step(i, carry):
        @pl.when(i < blocks)
        def _():
            for_sibling(i)

        @pl.when(i >= LEAD)
        def _():
            for_own(i - LEAD)

        return carry

    lax.fori_loop(0, blocks + LEAD, second_step, 0)
    pend.append(lambda: each(0, blocks, lambda k: snum_copy(k).wait_send()))
    pend.append(lambda: each(0, blocks, lambda k: stwo_copy(k).wait_send()))
    pend.append(lambda: each(0, half_blocks, lambda k: xnum_copy(k, k).wait_send()))
    pend.append(lambda: each(0, half_blocks, lambda k: xtwo_copy(k, k).wait_send()))
    pend.append(lambda: each(1, depth, lambda k: num_copy(r, z).wait_send()))
    pend.append(lambda: each(1, depth, lambda k: two_copy(0, r, z).wait_send()))
    got_two[z] = sum_two[r // 2]
    got_numer[z] = numer[part_at(r), :]
    each(1, depth, lambda k: two_copy(0, r, lax.rem(z + k, depth)).wait_recv())
    second = got_two[0]
    for q in range(1, depth):
        second = second + got_two[q]
    half = lax.rem(r, 2)
    pot_own = pot[pl.ds(home, 1), :]
    pot_own = jnp.where(half == lax.rem(t // 2, 2), pot_own, pltpu.roll(pot_own, PART, 1))
    pot_all[r] = 0.5 * (pot_own - 2.0 * (jnp.log(second) - log_count))

    def fin_copy(owner, target):
        return remote(
            pot_all.at[owner], pot_all.at[owner],
            send_sem.at[9], rv_fin.at[owner], {"rep": target},
        )

    each(1, reps, lambda k: fin_copy(r, rep_peer(k)).start())
    pend.append(lambda: each(1, reps, lambda k: fin_copy(r, r).wait_send()))
    lane = lax.broadcasted_iota(jnp.int32, (PART, LANES), 1)
    sub = lax.broadcasted_iota(jnp.int32, (PART, LANES), 0)
    divisor = jnp.sum(jnp.where(lane == sub + half * PART, second, 0.0), axis=1, keepdims=True)
    each(1, depth, lambda k: num_copy(r, lax.rem(z + k, depth)).wait_recv())
    weighted = got_numer[0]
    for q in range(1, depth):
        weighted = weighted + got_numer[q]
    disp_mine[...] = encode(pts[part_at(r), :].astype(jnp.float32) - weighted / divisor)

    def disp_copy(owner, target):
        return remote(
            disp_mine, disp_out.at[part_at(owner), :],
            send_sem.at[10], rv_disp.at[owner], {"rep": target},
        )

    def by_distance(j):
        k = j // 2 + 1
        return k + lax.rem(j, 2) * (depth - 2 * k)

    def send_disp(j):
        q = z_peer(by_distance(depth - 2 - j))
        disp_copy(r, lax.rem(q + depth, reps)).start()
        disp_copy(r, q).start()

    each(0, depth - 1, send_disp)
    disp_copy(r, across).start()
    pend.append(lambda: each(1, reps, lambda k: disp_copy(r, r).wait_send()))
    keep = pltpu.make_async_copy(disp_mine, disp_out.at[part_at(r), :], local_sem)
    keep.start()
    each(1, reps, lambda k: fin_copy(rep_peer(k), r).wait_recv())
    low_lane = lax.broadcasted_iota(jnp.int32, (1, LANES), 1) < PART
    for b in range(blocks):
        pot_out[b] = jnp.where(low_lane, pot_all[2 * b], pot_all[2 * b + 1])
    finish()
    each(1, reps, lambda k: disp_copy(rep_peer(k), r).wait_recv())
    keep.wait()


def shards(points):
    rows, width = points.shape
    teams = lax.axis_size("team")
    reps = lax.axis_size("rep")
    blocks = rows // LANES
    chips = teams // 2
    chunks = chips // 2
    depth = reps // 2
    f32 = jnp.float32
    dma = pltpu.SemaphoreType.DMA
    vmem = pltpu.VMEM
    potential, code = pl.pallas_call(
        functools.partial(body, teams, reps),
        out_shape=(
            jax.ShapeDtypeStruct((blocks, 1, LANES), f32),
            jax.ShapeDtypeStruct((rows, width), jnp.bfloat16),
        ),
        in_specs=[pl.BlockSpec(memory_space=pltpu.VMEM)],
        out_specs=(
            pl.BlockSpec(memory_space=pltpu.VMEM),
            pl.BlockSpec(memory_space=pl.ANY),
        ),
        scratch_shapes=[
            vmem((rows, width), jnp.bfloat16),
            vmem((2 * rows, 2 * width), jnp.bfloat16),
            vmem((chips * PART, width), jnp.bfloat16),
            vmem((chunks, 2 * rows, LANES), f32),
            vmem((chunks, LANES), f32),
            vmem((chips, chunks, LANES), f32),
            vmem((chunks, LANES), f32),
            vmem((chunks, LANES), f32),
            vmem((blocks, LANES, width), f32),
            vmem((blocks, 1, LANES), f32),
            vmem((blocks, LANES, width), f32),
            vmem((blocks, 1, LANES), f32),
            vmem((rows, width), f32),
            vmem((blocks, 1, LANES), f32),
            vmem((blocks // 2, LANES, width), f32),
            vmem((blocks // 2, 1, LANES), f32),
            vmem((depth, PART, width), f32),
            vmem((depth, 1, LANES), f32),
            vmem((PART, width), jnp.bfloat16),
            vmem((reps, 1, LANES), f32),
            dma((12,)),
            dma,
            dma,
            dma((chips,)),
            dma((chips,)),
            dma((blocks,)),
            dma((blocks,)),
            dma((blocks // 2,)),
            dma((blocks // 2,)),
            dma((depth,)),
            dma((depth,)),
            dma((reps,)),
            dma((reps,)),
        ],
        compiler_params=pltpu.CompilerParams(collective_id=0, has_side_effects=True),
    )(points)
    return potential.reshape(rows), decode(code)


def solution(mesh):
    return jax.shard_map(
        shards,
        mesh=mesh,
        in_specs=(P("team", None),),
        out_specs=(P("team"), P("team", None)),
        check_vma=False,
    )
```

```python
import functools
import math

import jax
import jax.numpy as jnp
from jax import lax
from jax.experimental import pallas as pl
from jax.experimental.pallas import tpu as pltpu
from jax.sharding import PartitionSpec as P

LANES = 128
PART = 64
LEAD = 2
MESH = pl.DeviceIdType.MESH
LOG2E = math.log2(math.e)


SCALE = 8192.0


def encode(value):
    power = value * SCALE
    for _ in range(3):
        power = power * power
    return jnp.where(value < 0.0, -power, power).astype(jnp.bfloat16)


def decode(code):
    power = code.astype(jnp.float32)
    size = jnp.exp2(jnp.log2(jnp.abs(power)) * 0.125) * (1.0 / SCALE)
    return jnp.where(power < 0.0, -size, size)


def split3(value):
    high = value.astype(jnp.bfloat16).astype(jnp.float32)
    rest = value - high
    mid = rest.astype(jnp.bfloat16).astype(jnp.float32)
    return high, mid, rest - mid


def extra_lanes(block, first, ones):
    wide = block.astype(jnp.float32)
    half = -0.5 * jnp.sum(wide * wide, axis=1, keepdims=True)
    high, mid, low = split3(half)
    lane = lax.broadcasted_iota(jnp.int32, wide.shape, 1)
    extra = jnp.where((lane >= ones) & (lane < ones + 3), 1.0, 0.0)
    extra = jnp.where(lane == first, high, extra)
    extra = jnp.where(lane == first + 1, mid, extra)
    extra = jnp.where(lane == first + 2, low, extra)
    return extra.astype(jnp.bfloat16)


def row_of(acc):
    size = acc.shape[0]
    total = jnp.sum(acc, axis=1, keepdims=True)
    lane = lax.broadcasted_iota(jnp.int32, (size, LANES), 1)
    sub = lax.broadcasted_iota(jnp.int32, (size, LANES), 0)
    return jnp.sum(jnp.where(lane == sub, total, 0.0), axis=0, keepdims=True)


def column_of(row, size, first):
    lane = lax.broadcasted_iota(jnp.int32, (size, LANES), 1)
    sub = lax.broadcasted_iota(jnp.int32, (size, LANES), 0)
    return jnp.sum(jnp.where(lane == sub + first, row, 0.0), axis=1, keepdims=True)


def body(
    teams, reps, pts, pot_out, disp_out,
    mate, rows_aug, cols, first_exp, chip_one, got_one, pot, weight,
    out_numer, out_two, sib_numer, sib_two,
    numer, sum_two, got_numer, got_two, disp_mine, pot_all,
    send_sem, local_sem, rv_mate, rv_pts, rv_one, rv_snum, rv_stwo,
    rv_num, rv_two, rv_disp, rv_fin,
):
    rows = pts.shape[0]
    blocks = rows // LANES
    chips = teams // 2
    chunks = chips // 2
    depth = reps // 2
    half_blocks = blocks // 2
    log_count = math.log(rows * teams)
    t = lax.axis_index("team")
    r = lax.axis_index("rep")
    core = lax.rem(t, 2)
    sibling = t + 1 - 2 * core
    near = r // depth
    z = lax.rem(r, depth)
    across = lax.rem(r + depth, reps)
    pairs = chunks // 2
    home = t // 4
    nt = (((1,), (1,)), ((), ()))

    def part_at(index):
        return pl.ds(pl.multiple_of(index * PART, PART), PART)

    def block_at(index):
        return pl.ds(pl.multiple_of(index * LANES, LANES), LANES)

    def remote(src, dst, send, recv, where):
        return pltpu.make_async_remote_copy(
            src_ref=src, dst_ref=dst, send_sem=send, recv_sem=recv,
            device_id=where, device_id_type=MESH,
        )

    def each(first, count, step):
        lax.fori_loop(first, count, lambda k, c: (step(k), c)[1], 0)

    def same_core(k):
        return lax.rem(t + 2 * k, teams)

    def rep_peer(k):
        return lax.rem(r + k, reps)

    def z_peer(k):
        return near * depth + lax.rem(z + k, depth)

    def chunk_of(i):
        side, step = lax.rem(i, 2), i // 2
        step = step + (step // 2) * (1 - 2 * lax.rem(step, 2))
        return lax.rem(home // pairs + side, 2) * pairs + lax.rem(home + step, pairs)

    pend = []

    def finish():
        for step in pend:
            step()

    barrier = pltpu.get_barrier_semaphore()

    def greet(where):
        pl.semaphore_signal(barrier, 1, device_id=where, device_id_type=MESH)

    each(1, chips, lambda k: greet({"team": same_core(k)}))
    greet({"team": sibling})
    each(1, reps, lambda k: greet({"rep": rep_peer(k)}))
    own = pltpu.make_async_copy(pts.at[part_at(r), :], cols.at[part_at(t // 2), :], local_sem)
    own.start()
    pl.semaphore_wait(barrier, chips + reps - 1)

    def points_copy(owner, target):
        return remote(
            pts.at[part_at(r), :], cols.at[part_at(owner), :],
            send_sem.at[0], rv_pts.at[owner], {"team": target},
        )

    def send_points(i, carry):
        for h in range(2):
            q = 4 * chunk_of(i) + 2 * h + core

            @pl.when(q != t)
            def _():
                points_copy(t // 2, q).start()

        return carry

    lax.fori_loop(0, chunks, send_points, 0)
    pend.append(lambda: each(1, chips, lambda k: points_copy(t // 2, t).wait_send()))
    mate_copy = remote(pts, mate, send_sem.at[1], rv_mate, {"team": sibling})
    mate_copy.start()
    pend.append(mate_copy.wait_send)
    own.wait()

    def widen_from(ref, first):
        def widen_rows(b, carry):
            block = ref[block_at(b), :]
            rows_aug[block_at(first + b), pl.ds(0, LANES)] = block
            rows_aug[block_at(first + b), pl.ds(LANES, LANES)] = extra_lanes(block, 0, 3)
            return carry

        lax.fori_loop(0, blocks, widen_rows, 0)

    widen_from(pts, 0)
    mate_copy.wait_recv()
    widen_from(mate, blocks)

    def first_chunk(i, carry):
        c = chunk_of(i)
        for h in range(2):
            k = 2 * c + h

            @pl.when(k != t // 2)
            def _():
                points_copy(k, t).wait_recv()

        block = cols[block_at(c), :]
        wide = jnp.concatenate([block, extra_lanes(block, 3, 0)], axis=1)
        acc = jnp.zeros((1, LANES), jnp.float32)
        for b in range(2 * rows // 256):
            tile = lax.dot_general(
                rows_aug[pl.ds(b * 256, 256), :], wide, nt, preferred_element_type=jnp.float32
            )
            tile = jnp.exp2(tile * (0.25 * LOG2E))
            first_exp[c, pl.ds(b * 256, 256), :] = tile
            acc = acc + jnp.sum(tile, axis=0, keepdims=True)
        chip_one[pl.ds(c, 1), :] = acc
        return carry

    lax.fori_loop(0, chunks, first_chunk, 0)

    def one_copy(owner, target):
        return remote(
            chip_one, got_one.at[owner], send_sem.at[3], rv_one.at[owner], {"team": target}
        )

    each(1, chips, lambda k: one_copy(t // 2, same_core(k)).start())
    pend.append(lambda: each(1, chips, lambda k: one_copy(0, t).wait_send()))
    got_one[t // 2] = chip_one[...]
    each(1, chips, lambda k: one_copy(same_core(k) // 2, t).wait_recv())
    first = got_one[0]
    for q in range(1, chips):
        first = first + got_one[q]
    pot[...] = -2.0 * (jnp.log(first) - log_count)

    weight[...] = jnp.exp2(pot[...] * (0.5 * LOG2E))

    def second_block(b):
        acc = jnp.zeros((LANES, LANES), jnp.float32)
        total = jnp.zeros((LANES, LANES), jnp.float32)
        for s in range(chunks // 2):
            left = first_exp[2 * s, block_at(b), :]
            left = left * weight[2 * s : 2 * s + 1, :] * left
            right = first_exp[2 * s + 1, block_at(b), :]
            right = right * weight[2 * s + 1 : 2 * s + 2, :] * right
            acc = acc + left + right
            rounded = jnp.concatenate(
                [left.astype(jnp.bfloat16), right.astype(jnp.bfloat16)], axis=1
            )
            total = total + jnp.dot(
                rounded, cols[pl.ds(s * 256, 256), :], preferred_element_type=jnp.float32
            )
        return row_of(acc), total

    def snum_copy(b):
        return remote(
            out_numer.at[b], sib_numer.at[b], send_sem.at[2], rv_snum.at[b], {"team": sibling}
        )

    def stwo_copy(b):
        return remote(
            out_two.at[b], sib_two.at[b], send_sem.at[4], rv_stwo.at[b], {"team": sibling}
        )

    def turn(i):
        return lax.rem(z // 2 + 2 - i + (i // 2) * (7 - 2 * i) + half_blocks, half_blocks)

    def num_copy(dest, owner):
        return remote(
            numer.at[part_at(dest), :], got_numer.at[owner],
            send_sem.at[7], rv_num.at[owner], {"rep": dest},
        )

    def two_copy(b, dest, owner):
        return remote(
            sum_two.at[b], got_two.at[owner],
            send_sem.at[8], rv_two.at[owner], {"rep": dest},
        )

    def place(i):
        return lax.rem(1 - near + i, 2) * half_blocks + turn(i // 2)

    def for_sibling(i):
        b = place(i)
        row, total = second_block(blocks + b)
        out_numer[b] = total
        out_two[b] = row
        snum_copy(b).start()
        stwo_copy(b).start()

    def for_own(i):
        b = place(i)
        row, total = second_block(b)
        snum_copy(b).wait_recv()
        stwo_copy(b).wait_recv()
        row = row + sib_two[b]
        sum_two[b] = row
        mean = (total + sib_numer[b]) / jnp.maximum(column_of(row, LANES, 0), 1e-30)
        numer[block_at(b), :] = encode(pts[block_at(b), :].astype(jnp.float32) - mean)
        for h in range(2):
            q = 2 * b + h

            @pl.when(q != r)
            def _():
                two_copy(b, q, r).start()
                num_copy(q, r).start()

    def second_step(i, carry):
        @pl.when(i < blocks)
        def _():
            for_sibling(i)

        @pl.when(i >= LEAD)
        def _():
            for_own(i - LEAD)

        return carry

    lax.fori_loop(0, blocks + LEAD, second_step, 0)
    pend.append(lambda: each(0, blocks, lambda k: snum_copy(k).wait_send()))
    pend.append(lambda: each(0, blocks, lambda k: stwo_copy(k).wait_send()))
    pend.append(lambda: each(1, reps, lambda k: num_copy(r, r).wait_send()))
    pend.append(lambda: each(1, reps, lambda k: two_copy(0, r, r).wait_send()))
    got_two[r] = sum_two[r // 2]
    got_numer[r] = numer[part_at(r), :]
    each(1, reps, lambda k: two_copy(0, r, rep_peer(k)).wait_recv())
    second = got_two[0]
    for q in range(1, reps):
        second = second + got_two[q]
    half = lax.rem(r, 2)
    pot_own = pot[pl.ds(home, 1), :]
    pot_own = jnp.where(half == lax.rem(t // 2, 2), pot_own, pltpu.roll(pot_own, PART, 1))
    pot_all[r] = 0.5 * (pot_own - 2.0 * (jnp.log(second) - log_count))

    def fin_copy(owner, target):
        return remote(
            pot_all.at[owner], pot_all.at[owner],
            send_sem.at[9], rv_fin.at[owner], {"rep": target},
        )

    each(1, reps, lambda k: fin_copy(r, rep_peer(k)).start())
    pend.append(lambda: each(1, reps, lambda k: fin_copy(r, r).wait_send()))
    divisor = column_of(second, PART, half * PART)
    shares = [column_of(got_two[q], PART, half * PART) / divisor for q in range(reps)]
    each(1, reps, lambda k: num_copy(r, rep_peer(k)).wait_recv())
    moved = decode(got_numer[0]) * shares[0]
    for q in range(1, reps):
        moved = moved + decode(got_numer[q]) * shares[q]
    disp_mine[...] = encode(moved)

    def disp_copy(owner, target):
        return remote(
            disp_mine, disp_out.at[part_at(owner), :],
            send_sem.at[10], rv_disp.at[owner], {"rep": target},
        )

    def by_distance(j):
        k = j // 2 + 1
        return k + lax.rem(j, 2) * (depth - 2 * k)

    def send_disp(j):
        q = z_peer(by_distance(depth - 2 - j))
        disp_copy(r, lax.rem(q + depth, reps)).start()
        disp_copy(r, q).start()

    each(0, depth - 1, send_disp)
    disp_copy(r, across).start()
    pend.append(lambda: each(1, reps, lambda k: disp_copy(r, r).wait_send()))
    keep = pltpu.make_async_copy(disp_mine, disp_out.at[part_at(r), :], local_sem)
    keep.start()
    each(1, reps, lambda k: fin_copy(rep_peer(k), r).wait_recv())
    low_lane = lax.broadcasted_iota(jnp.int32, (1, LANES), 1) < PART
    for b in range(blocks):
        pot_out[pl.ds(b, 1), :] = jnp.where(low_lane, pot_all[2 * b], pot_all[2 * b + 1])
    finish()
    each(1, reps, lambda k: disp_copy(rep_peer(k), r).wait_recv())
    keep.wait()


def shards(points):
    rows, width = points.shape
    teams = lax.axis_size("team")
    reps = lax.axis_size("rep")
    blocks = rows // LANES
    chips = teams // 2
    chunks = chips // 2
    depth = reps // 2
    f32 = jnp.float32
    dma = pltpu.SemaphoreType.DMA
    vmem = pltpu.VMEM
    potential, code = pl.pallas_call(
        functools.partial(body, teams, reps),
        out_shape=(
            jax.ShapeDtypeStruct((blocks, LANES), f32),
            jax.ShapeDtypeStruct((rows, width), jnp.bfloat16),
        ),
        in_specs=[pl.BlockSpec(memory_space=pltpu.VMEM)],
        out_specs=(
            pl.BlockSpec(memory_space=pltpu.VMEM),
            pl.BlockSpec(memory_space=pl.ANY),
        ),
        scratch_shapes=[
            vmem((rows, width), jnp.bfloat16),
            vmem((2 * rows, 2 * width), jnp.bfloat16),
            vmem((chips * PART, width), jnp.bfloat16),
            vmem((chunks, 2 * rows, LANES), f32),
            vmem((chunks, LANES), f32),
            vmem((chips, chunks, LANES), f32),
            vmem((chunks, LANES), f32),
            vmem((chunks, LANES), f32),
            vmem((blocks, LANES, width), f32),
            vmem((blocks, 1, LANES), f32),
            vmem((blocks, LANES, width), f32),
            vmem((blocks, 1, LANES), f32),
            vmem((rows, width), jnp.bfloat16),
            vmem((blocks, 1, LANES), f32),
            vmem((reps, PART, width), jnp.bfloat16),
            vmem((reps, 1, LANES), f32),
            vmem((PART, width), jnp.bfloat16),
            vmem((reps, 1, LANES), f32),
            dma((12,)),
            dma,
            dma,
            dma((chips,)),
            dma((chips,)),
            dma((blocks,)),
            dma((blocks,)),
            dma((reps,)),
            dma((reps,)),
            dma((reps,)),
            dma((reps,)),
        ],
        compiler_params=pltpu.CompilerParams(collective_id=0, has_side_effects=True),
    )(points)
    return potential.reshape(rows), decode(code)


def solution(mesh):
    return jax.shard_map(
        shards,
        mesh=mesh,
        in_specs=(P("team", None),),
        out_specs=(P("team"), P("team", None)),
        check_vma=False,
    )
```

```python
import functools
import math

import jax
import jax.numpy as jnp
from jax import lax
from jax.experimental import pallas as pl
from jax.experimental.pallas import tpu as pltpu
from jax.sharding import PartitionSpec as P

LANES = 128
PART = 64
LEAD = 2
MESH = pl.DeviceIdType.MESH
LOG2E = math.log2(math.e)


SCALE = 8192.0


def encode(value):
    power = value * SCALE
    for _ in range(3):
        power = power * power
    return jnp.where(value < 0.0, -power, power).astype(jnp.bfloat16)


def decode(code):
    power = code.astype(jnp.float32)
    size = jnp.exp2(jnp.log2(jnp.abs(power)) * 0.125) * (1.0 / SCALE)
    return jnp.where(power < 0.0, -size, size)


def split3(value):
    high = value.astype(jnp.bfloat16).astype(jnp.float32)
    rest = value - high
    mid = rest.astype(jnp.bfloat16).astype(jnp.float32)
    return high, mid, rest - mid


def extra_lanes(block, first, ones):
    wide = block.astype(jnp.float32)
    half = -0.5 * jnp.sum(wide * wide, axis=1, keepdims=True)
    high, mid, low = split3(half)
    lane = lax.broadcasted_iota(jnp.int32, wide.shape, 1)
    extra = jnp.where((lane >= ones) & (lane < ones + 3), 1.0, 0.0)
    extra = jnp.where(lane == first, high, extra)
    extra = jnp.where(lane == first + 1, mid, extra)
    extra = jnp.where(lane == first + 2, low, extra)
    return extra.astype(jnp.bfloat16)


def row_of(acc):
    size = acc.shape[0]
    total = jnp.sum(acc, axis=1, keepdims=True)
    lane = lax.broadcasted_iota(jnp.int32, (size, LANES), 1)
    sub = lax.broadcasted_iota(jnp.int32, (size, LANES), 0)
    return jnp.sum(jnp.where(lane == sub, total, 0.0), axis=0, keepdims=True)


def column_of(row, size, first):
    lane = lax.broadcasted_iota(jnp.int32, (size, LANES), 1)
    sub = lax.broadcasted_iota(jnp.int32, (size, LANES), 0)
    return jnp.sum(jnp.where(lane == sub + first, row, 0.0), axis=1, keepdims=True)


def body(
    teams, reps, source, pot_out, disp_out,
    pts,
    mate, rows_aug, cols, first_exp, chip_one, got_one, pot, weight,
    out_numer, out_two, sib_numer, sib_two,
    numer, sum_two, got_numer, got_two, disp_mine, pot_all,
    send_sem, local_sem, rv_mate, rv_pts, rv_one, rv_snum, rv_stwo,
    rv_num, rv_two, rv_disp, rv_fin,
):
    rows = pts.shape[0]
    blocks = rows // LANES
    chips = teams // 2
    chunks = chips // 2
    depth = reps // 2
    half_blocks = blocks // 2
    log_count = math.log(rows * teams)
    t = lax.axis_index("team")
    r = lax.axis_index("rep")
    core = lax.rem(t, 2)
    sibling = t + 1 - 2 * core
    near = r // depth
    z = lax.rem(r, depth)
    across = lax.rem(r + depth, reps)
    pairs = chunks // 2
    home = t // 4
    nt = (((1,), (1,)), ((), ()))

    def part_at(index):
        return pl.ds(pl.multiple_of(index * PART, PART), PART)

    def block_at(index):
        return pl.ds(pl.multiple_of(index * LANES, LANES), LANES)

    def remote(src, dst, send, recv, where):
        return pltpu.make_async_remote_copy(
            src_ref=src, dst_ref=dst, send_sem=send, recv_sem=recv,
            device_id=where, device_id_type=MESH,
        )

    def each(first, count, step):
        lax.fori_loop(first, count, lambda k, c: (step(k), c)[1], 0)

    def same_core(k):
        return lax.rem(t + 2 * k, teams)

    def rep_peer(k):
        return lax.rem(r + k, reps)

    def z_peer(k):
        return near * depth + lax.rem(z + k, depth)

    def chunk_of(i):
        side, step = lax.rem(i, 2), i // 2
        step = step + (step // 2) * (1 - 2 * lax.rem(step, 2))
        return lax.rem(home // pairs + side, 2) * pairs + lax.rem(home + step, pairs)

    pend = []

    def finish():
        for step in pend:
            step()

    barrier = pltpu.get_barrier_semaphore()

    def greet(where):
        pl.semaphore_signal(barrier, 1, device_id=where, device_id_type=MESH)

    each(1, chips, lambda k: greet({"team": same_core(k)}))
    greet({"team": sibling})
    each(1, reps, lambda k: greet({"rep": rep_peer(k)}))
    own = pltpu.make_async_copy(
        source.at[part_at(r), :], cols.at[part_at(t // 2), :], local_sem.at[0]
    )
    own.start()
    load = pltpu.make_async_copy(source, pts, local_sem.at[1])
    load.start()
    pl.semaphore_wait(barrier, chips + reps - 1)

    def points_copy(owner, target):
        return remote(
            source.at[part_at(r), :], cols.at[part_at(owner), :],
            send_sem.at[0], rv_pts.at[owner], {"team": target},
        )

    def send_points(i, carry):
        for h in range(2):
            q = 4 * chunk_of(i) + 2 * h + core

            @pl.when(q != t)
            def _():
                points_copy(t // 2, q).start()

        return carry

    lax.fori_loop(0, chunks, send_points, 0)
    pend.append(lambda: each(1, chips, lambda k: points_copy(t // 2, t).wait_send()))
    mate_copy = remote(source, mate, send_sem.at[1], rv_mate, {"team": sibling})
    mate_copy.start()
    pend.append(mate_copy.wait_send)
    own.wait()
    load.wait()

    def widen_from(ref, first):
        def widen_rows(b, carry):
            block = ref[block_at(b), :]
            rows_aug[block_at(first + b), pl.ds(0, LANES)] = block
            rows_aug[block_at(first + b), pl.ds(LANES, LANES)] = extra_lanes(block, 0, 3)
            return carry

        lax.fori_loop(0, blocks, widen_rows, 0)

    widen_from(pts, 0)
    mate_copy.wait_recv()
    widen_from(mate, blocks)

    def first_chunk(i, carry):
        c = chunk_of(i)
        for h in range(2):
            k = 2 * c + h

            @pl.when(k != t // 2)
            def _():
                points_copy(k, t).wait_recv()

        block = cols[block_at(c), :]
        wide = jnp.concatenate([block, extra_lanes(block, 3, 0)], axis=1)
        acc = jnp.zeros((1, LANES), jnp.float32)
        for b in range(2 * rows // 256):
            tile = lax.dot_general(
                rows_aug[pl.ds(b * 256, 256), :], wide, nt, preferred_element_type=jnp.float32
            )
            tile = jnp.exp2(tile * (0.25 * LOG2E))
            first_exp[c, pl.ds(b * 256, 256), :] = tile
            acc = acc + jnp.sum(tile, axis=0, keepdims=True)
        chip_one[pl.ds(c, 1), :] = acc
        return carry

    lax.fori_loop(0, chunks, first_chunk, 0)

    def one_copy(owner, target):
        return remote(
            chip_one, got_one.at[owner], send_sem.at[3], rv_one.at[owner], {"team": target}
        )

    each(1, chips, lambda k: one_copy(t // 2, same_core(k)).start())
    pend.append(lambda: each(1, chips, lambda k: one_copy(0, t).wait_send()))
    got_one[t // 2] = chip_one[...]
    each(1, chips, lambda k: one_copy(same_core(k) // 2, t).wait_recv())
    first = got_one[0]
    for q in range(1, chips):
        first = first + got_one[q]
    pot[...] = -2.0 * (jnp.log(first) - log_count)

    weight[...] = jnp.exp2(pot[...] * (0.5 * LOG2E))

    def second_block(b):
        acc = jnp.zeros((LANES, LANES), jnp.float32)
        total = jnp.zeros((LANES, LANES), jnp.float32)
        for s in range(chunks // 2):
            left = first_exp[2 * s, block_at(b), :]
            left = left * weight[2 * s : 2 * s + 1, :] * left
            right = first_exp[2 * s + 1, block_at(b), :]
            right = right * weight[2 * s + 1 : 2 * s + 2, :] * right
            acc = acc + left + right
            rounded = jnp.concatenate(
                [left.astype(jnp.bfloat16), right.astype(jnp.bfloat16)], axis=1
            )
            total = total + jnp.dot(
                rounded, cols[pl.ds(s * 256, 256), :], preferred_element_type=jnp.float32
            )
        return row_of(acc), total

    def snum_copy(b):
        return remote(
            out_numer.at[b], sib_numer.at[b], send_sem.at[2], rv_snum.at[b], {"team": sibling}
        )

    def stwo_copy(b):
        return remote(
            out_two.at[b], sib_two.at[b], send_sem.at[4], rv_stwo.at[b], {"team": sibling}
        )

    def turn(i):
        return lax.rem(z // 2 + 2 - i + (i // 2) * (7 - 2 * i) + half_blocks, half_blocks)

    def num_copy(dest, owner):
        return remote(
            numer.at[part_at(dest), :], got_numer.at[owner],
            send_sem.at[7], rv_num.at[owner], {"rep": dest},
        )

    def two_copy(b, dest, owner):
        return remote(
            sum_two.at[b], got_two.at[owner],
            send_sem.at[8], rv_two.at[owner], {"rep": dest},
        )

    def place(i):
        return lax.rem(1 - near + i, 2) * half_blocks + turn(i // 2)

    def for_sibling(i):
        b = place(i)
        row, total = second_block(blocks + b)
        out_numer[b] = total
        out_two[b] = row
        snum_copy(b).start()
        stwo_copy(b).start()

    def for_own(i):
        b = place(i)
        row, total = second_block(b)
        snum_copy(b).wait_recv()
        stwo_copy(b).wait_recv()
        row = row + sib_two[b]
        sum_two[b] = row
        mean = (total + sib_numer[b]) / jnp.maximum(column_of(row, LANES, 0), 1e-30)
        numer[block_at(b), :] = encode(pts[block_at(b), :].astype(jnp.float32) - mean)
        for h in range(2):
            q = 2 * b + h

            @pl.when(q != r)
            def _():
                two_copy(b, q, r).start()
                num_copy(q, r).start()

    def second_step(i, carry):
        @pl.when(i < blocks)
        def _():
            for_sibling(i)

        @pl.when(i >= LEAD)
        def _():
            for_own(i - LEAD)

        return carry

    lax.fori_loop(0, blocks + LEAD, second_step, 0)
    pend.append(lambda: each(0, blocks, lambda k: snum_copy(k).wait_send()))
    pend.append(lambda: each(0, blocks, lambda k: stwo_copy(k).wait_send()))
    pend.append(lambda: each(1, reps, lambda k: num_copy(r, r).wait_send()))
    pend.append(lambda: each(1, reps, lambda k: two_copy(0, r, r).wait_send()))
    got_two[r] = sum_two[r // 2]
    got_numer[r] = numer[part_at(r), :]
    each(1, reps, lambda k: two_copy(0, r, rep_peer(k)).wait_recv())
    second = got_two[0]
    for q in range(1, reps):
        second = second + got_two[q]
    half = lax.rem(r, 2)
    pot_own = pot[pl.ds(home, 1), :]
    pot_own = jnp.where(half == lax.rem(t // 2, 2), pot_own, pltpu.roll(pot_own, PART, 1))
    pot_all[r] = 0.5 * (pot_own - 2.0 * (jnp.log(second) - log_count))

    def fin_copy(owner, target):
        return remote(
            pot_all.at[owner], pot_all.at[owner],
            send_sem.at[9], rv_fin.at[owner], {"rep": target},
        )

    each(1, reps, lambda k: fin_copy(r, rep_peer(k)).start())
    pend.append(lambda: each(1, reps, lambda k: fin_copy(r, r).wait_send()))
    divisor = column_of(second, PART, half * PART)
    shares = [column_of(got_two[q], PART, half * PART) / divisor for q in range(reps)]
    each(1, reps, lambda k: num_copy(r, rep_peer(k)).wait_recv())
    moved = decode(got_numer[0]) * shares[0]
    for q in range(1, reps):
        moved = moved + decode(got_numer[q]) * shares[q]
    disp_mine[...] = encode(moved)

    def disp_copy(owner, target):
        return remote(
            disp_mine, disp_out.at[part_at(owner), :],
            send_sem.at[10], rv_disp.at[owner], {"rep": target},
        )

    def by_distance(j):
        k = j // 2 + 1
        return k + lax.rem(j, 2) * (depth - 2 * k)

    def send_disp(j):
        q = z_peer(by_distance(depth - 2 - j))
        disp_copy(r, lax.rem(q + depth, reps)).start()
        disp_copy(r, q).start()

    each(0, depth - 1, send_disp)
    disp_copy(r, across).start()
    pend.append(lambda: each(1, reps, lambda k: disp_copy(r, r).wait_send()))
    keep = pltpu.make_async_copy(disp_mine, disp_out.at[part_at(r), :], local_sem.at[0])
    keep.start()
    each(1, reps, lambda k: fin_copy(rep_peer(k), r).wait_recv())
    low_lane = lax.broadcasted_iota(jnp.int32, (1, LANES), 1) < PART
    for b in range(blocks):
        pot_out[pl.ds(b, 1), :] = jnp.where(low_lane, pot_all[2 * b], pot_all[2 * b + 1])
    finish()
    each(1, reps, lambda k: disp_copy(rep_peer(k), r).wait_recv())
    keep.wait()


def finish_body(pot, code, pot_out, disp_out):
    pot_out[...] = pot[...]
    disp_out[...] = decode(code[...])


def shards(points):
    rows, width = points.shape
    teams = lax.axis_size("team")
    reps = lax.axis_size("rep")
    blocks = rows // LANES
    chips = teams // 2
    chunks = chips // 2
    depth = reps // 2
    f32 = jnp.float32
    dma = pltpu.SemaphoreType.DMA
    vmem = pltpu.VMEM
    potential, code = pl.pallas_call(
        functools.partial(body, teams, reps),
        out_shape=(
            jax.ShapeDtypeStruct((blocks, LANES), f32),
            jax.ShapeDtypeStruct((rows, width), jnp.bfloat16),
        ),
        in_specs=[pl.BlockSpec(memory_space=pl.ANY)],
        out_specs=(
            pl.BlockSpec(memory_space=pltpu.VMEM),
            pl.BlockSpec(memory_space=pl.ANY),
        ),
        scratch_shapes=[
            vmem((rows, width), jnp.bfloat16),
            vmem((rows, width), jnp.bfloat16),
            vmem((2 * rows, 2 * width), jnp.bfloat16),
            vmem((chips * PART, width), jnp.bfloat16),
            vmem((chunks, 2 * rows, LANES), f32),
            vmem((chunks, LANES), f32),
            vmem((chips, chunks, LANES), f32),
            vmem((chunks, LANES), f32),
            vmem((chunks, LANES), f32),
            vmem((blocks, LANES, width), f32),
            vmem((blocks, 1, LANES), f32),
            vmem((blocks, LANES, width), f32),
            vmem((blocks, 1, LANES), f32),
            vmem((rows, width), jnp.bfloat16),
            vmem((blocks, 1, LANES), f32),
            vmem((reps, PART, width), jnp.bfloat16),
            vmem((reps, 1, LANES), f32),
            vmem((PART, width), jnp.bfloat16),
            vmem((reps, 1, LANES), f32),
            dma((12,)),
            dma((2,)),
            dma,
            dma((chips,)),
            dma((chips,)),
            dma((blocks,)),
            dma((blocks,)),
            dma((reps,)),
            dma((reps,)),
            dma((reps,)),
            dma((reps,)),
        ],
        compiler_params=pltpu.CompilerParams(collective_id=0, has_side_effects=True),
    )(points)
    potential, displacement = pl.pallas_call(
        finish_body,
        grid=(2,),
        out_shape=(
            jax.ShapeDtypeStruct((blocks, LANES), f32),
            jax.ShapeDtypeStruct((rows, width), f32),
        ),
        in_specs=[
            pl.BlockSpec((blocks, LANES), lambda i: (0, 0)),
            pl.BlockSpec((rows // 2, width), lambda i: (i, 0)),
        ],
        out_specs=(
            pl.BlockSpec((blocks, LANES), lambda i: (0, 0)),
            pl.BlockSpec((rows // 2, width), lambda i: (i, 0)),
        ),
    )(potential, code)
    return potential.reshape(rows), displacement


def solution(mesh):
    return jax.shard_map(
        shards,
        mesh=mesh,
        in_specs=(P("team", None),),
        out_specs=(P("team"), P("team", None)),
        check_vma=False,
    )
```
